32 devices in a mesh: dp: 2 (over core), ctx: 4 (over z), tp: 4 (over y, x).
Axes of the slice: x: 2, y: 2, z: 4, core: 2. Of those that a mesh axis runs over, the one named last changes fastest.
Arguments:
- projected: bfloat16 [2, 3, 512, 4096], P('dp', None, 'ctx', 'tp'), may hold values from -6 to 6
- cotangent: bfloat16 [2, 512, 4096], P('dp', 'ctx', 'tp'), may hold values from -6 to 6
- conv_taps: float32 [3, 7, 4096], P(None, None, 'tp'), may hold values from -2 to 2
- residues: float32 [16, 4096], P(None, 'tp'), may hold values from -1.5 to 1.5
- decay_rates: float32 [16, 4096], P(None, 'tp'), may hold values from 0.00048828125 to 0.0625, as said below
- skip_gain: float32 [4096], P('tp'), may hold values from 0.1 to 1.9
Outputs:
- mixed: bfloat16 [2, 512, 4096], P('dp', 'ctx', 'tp')
- input_grad: bfloat16 [2, 3, 512, 4096], P('dp', None, 'ctx', 'tp')
- taps_update: float32 [3, 7, 4096], P(None, None, 'tp')
- residue_update: float32 [16, 4096], P(None, 'tp')
- rate_update: float32 [16, 4096], P(None, 'tp')
- skip_update: float32 [4096], P('tp')
The draws below stay inside these ranges and needn't reach their ends.
Inputs may be any that keep to these rules, and one draw needn't show every extreme that they name: `decay_rates`: decay rates of the poles; positive.
All inputs are finite; a program needn't handle non-finite values.
Results may differ from the reference program's by a relative error of at most 0.0013.
Values may be sent and summed in bfloat16 or wider, within the bound.
A program may use at most 64 MiB of HBM per device.

```python
import math
import jax
import jax.numpy as jnp
from jax import lax

D = 4096
ORDER = 16
SHORT = 7
TOK_DEV = 128
SEQ = 512
BATCH = 2


def draw_decay_rates(key, part):
    level_key = jax.random.fold_in(jax.random.fold_in(key, 17), 1)
    spot = jax.random.uniform(level_key, (ORDER, D), jnp.float32)
    lowest = math.log(0.25 / SEQ)
    highest = math.log(1.0 / 16.0)
    return jnp.exp(lowest + spot * (highest - lowest))


def steps_of(own_key, shape, cuts, least, largest):
    def one(axis_at, blocks):
        heights = jax.random.uniform(jax.random.fold_in(jax.random.fold_in(own_key, 6), axis_at), (blocks,), jnp.float32, least / len(cuts), largest / len(cuts))
        return jnp.repeat(jnp.exp(heights), shape[axis_at] // blocks).reshape((-1,) + (1,) * (len(shape) - axis_at - 1))

    loudness = one(*cuts[0])
    for cut in cuts[1:]:
        loudness = loudness * one(*cut)
    return loudness


def scatter_about(stream_key, dims, scale, bound, pieces=(), dtype=jnp.bfloat16):
    factor_of = steps_of(stream_key, dims, pieces, -0.22, 0.18) if pieces else 1.0
    result = jax.random.normal(stream_key, dims, jnp.float32) * scale * factor_of
    return jnp.minimum(jnp.maximum(result, -bound), bound).astype(dtype)


def setup_inputs(seed: int = 0) -> dict:
    arg_keys = jax.random.split(jax.random.key(seed), 7)
    return {
        "projected": scatter_about(arg_keys[0], (BATCH, 3, SEQ, D), 1.0, 6.0, ((0, 2), (2, 4), (3, 4))),
        "cotangent": scatter_about(arg_keys[1], (BATCH, SEQ, D), 1.0, 6.0, ((0, 2), (1, 4), (2, 4))),
        "conv_taps": scatter_about(arg_keys[2], (3, SHORT, D), SHORT ** -0.5, 2.0, ((2, 4),), jnp.float32),
        "residues": scatter_about(arg_keys[3], (ORDER, D), 0.25, 1.5, ((1, 4),), jnp.float32),
        "decay_rates": draw_decay_rates(jax.random.fold_in(arg_keys[6], 71), 0),
        "skip_gain": jnp.clip(1.0 + 0.18 * jax.random.normal(arg_keys[5], (D,), jnp.float32), 0.1, 1.9),
    }


def modal_block(carried, block, decays, coeffs):

    def advance(state_now, drive_row):
        state_now = decays * state_now + drive_row[None, :]
        return (state_now, lax.optimization_barrier(jnp.sum(coeffs * state_now, axis=0)))
    return lax.scan(advance, carried, block)

def forward(streams, conv_taps, residues, decay_rates, skip_gain):
    edge = SHORT - 1
    padded = jnp.pad(streams, ((0, 0), (edge, 0), (0, 0)))
    features = sum((conv_taps[:, offset, None, :] * padded[:, edge - offset:edge - offset + SEQ, :] for offset in range(SHORT)))
    drive = features[1] * features[2]
    decays = jnp.exp(-decay_rates)
    coeffs = residues * jnp.sqrt(-jnp.expm1(-2.0 * decay_rates))
    blocks = drive.reshape(SEQ // TOK_DEV, TOK_DEV, D)

    def per_block(carried, block):
        return modal_block(carried, block, decays, coeffs)
    _, long_term = lax.scan(jax.checkpoint(per_block), jnp.zeros((ORDER, D), jnp.float32), blocks)
    long_term = long_term.reshape(SEQ, D)
    return features[0] * (long_term + skip_gain * drive)

def clipped(grad_value):
    return grad_value / jnp.maximum(1.0, jnp.sqrt(jnp.mean(grad_value * grad_value)))

def reference(projected, cotangent, conv_taps, residues, decay_rates, skip_gain):
    outputs = []
    in_grads = []
    param_grads = None
    for batch_row in range(BATCH):
        mixed_row, pullback = jax.vjp(forward, projected[batch_row].astype(jnp.float32), conv_taps, residues, decay_rates, skip_gain)
        grads = pullback(cotangent[batch_row].astype(jnp.float32))
        outputs.append(mixed_row.astype(jnp.bfloat16))
        in_grads.append(grads[0].astype(jnp.bfloat16))
        if param_grads is None:
            param_grads = list(grads[1:])
        else:
            param_grads = [total + extra for total, extra in zip(param_grads, grads[1:])]
    mixed = jnp.stack(outputs, axis=0)
    input_grad = jnp.stack(in_grads, axis=0)
    return (mixed, input_grad, clipped(param_grads[0]), clipped(param_grads[1]), clipped(param_grads[2]), clipped(param_grads[3]))
```

```python
import functools
import jax
import jax.numpy as jnp
from jax import lax
from jax.experimental import pallas as pl
from jax.experimental.pallas import tpu as pltpu
from jax.sharding import PartitionSpec as P


def prefix(x, axis, combine, identity, reverse):
    peers, mine = (lax.axis_size(axis), lax.axis_index(axis))
    everything = jax.tree.map(lambda part: lax.all_gather(part, axis), x)
    start = jax.tree.map(
        lambda part, zero: jnp.broadcast_to(jnp.asarray(zero, part.dtype), part.shape), x, identity
    )

    def step(k, before):
        at = peers - 1 - k if reverse else k
        reached = at > mine if reverse else at < mine
        new = combine(before, jax.tree.map(lambda part: part[at], everything))
        return jax.tree.map(lambda a, b: jnp.where(reached, a, b), new, before)

    return lax.fori_loop(0, peers, step, start)


def shifted(block, axis, distance):
    devices = range(lax.axis_size(axis))
    route = [(i - distance, i) for i in devices if i - distance in devices]
    return lax.ppermute(block, axis, route)


def linear_combine(earlier, later):
    return (earlier[0] * later[0], later[0] * earlier[1] + later[1])


def carry_pass(block_decay, summary, backward):
    identity = (jnp.ones_like(summary), jnp.zeros_like(summary))
    return prefix((block_decay, summary), "ctx", linear_combine, identity, backward)[1]


def local(projected, cotangent, conv_taps, residues, decay_rates, skip_gain):
    streams = projected[0]
    tok_rows = streams.shape[1]
    width = streams.shape[2]
    order = residues.shape[0]
    tap_count = conv_taps.shape[1]
    edge_rows = tap_count - 1
    prev_rows = shifted(streams[:, tok_rows - edge_rows :, :], "ctx", 1)
    padded = jnp.concatenate([prev_rows, streams], axis=1).astype(jnp.float32)
    features = conv_taps[:, 0, None, :] * padded[:, edge_rows : edge_rows + tok_rows, :]
    for offset in range(1, tap_count):
        features = (
            features
            + conv_taps[:, offset, None, :]
            * padded[:, edge_rows - offset : edge_rows - offset + tok_rows, :]
        )
    query = features[0]
    keyed = features[1]
    valued = features[2]
    drive = keyed * valued
    decays = jnp.exp(-decay_rates)
    root_norm = jnp.sqrt(-jnp.expm1(-2.0 * decay_rates))
    coeffs = residues * root_norm
    cot_rows = cotangent[0].astype(jnp.float32)
    grad_z = cot_rows * query
    zeros_state = jnp.zeros((order, width), jnp.float32)

    def local_step(carried, rows):
        state_now, adj_now = carried
        drive_row, grad_row = rows
        state_now = decays * state_now + drive_row[None, :]
        adj_now = decays * adj_now + coeffs * grad_row[None, :]
        return ((state_now, adj_now), None)

    (end_state, first_adjoint), _ = lax.scan(
        local_step, (zeros_state, zeros_state), (drive, grad_z[::-1]), unroll=8
    )
    block_decay = jnp.exp(-decay_rates * tok_rows)
    state_in = carry_pass(block_decay, end_state, False)
    adjoint_in = carry_pass(block_decay, first_adjoint, True)

    def forward_step(carried, rows):
        state_now, coeff_acc = carried
        drive_row, grad_row = rows
        before = state_now
        state_now = decays * state_now + drive_row[None, :]
        coeff_acc = coeff_acc + grad_row[None, :] * state_now
        return ((state_now, coeff_acc), (before, jnp.sum(coeffs * state_now, axis=0)))

    (_, coeff_grad), (state_prev, long_term) = lax.scan(
        forward_step, (state_in, zeros_state), (drive, grad_z), unroll=8
    )

    def backward_step(carried, rows):
        adj_now, decay_acc = carried
        grad_row, before = rows
        adj_now = decays * adj_now + coeffs * grad_row[None, :]
        decay_acc = decay_acc + adj_now * before
        return ((adj_now, decay_acc), jnp.sum(adj_now, axis=0))

    (_, decay_grad), adjoint_total = lax.scan(
        backward_step, (adjoint_in, zeros_state), (grad_z, state_prev), reverse=True, unroll=8
    )
    mixer_out = long_term + skip_gain * drive
    mixed = (query * mixer_out).astype(jnp.bfloat16)[None]
    grad_drive = adjoint_total + skip_gain * grad_z
    feature_grad = jnp.stack(
        [cot_rows * mixer_out, grad_drive * valued, grad_drive * keyed], axis=0
    )
    next_rows = shifted(feature_grad[:, :edge_rows, :], "ctx", -1)
    grad_padded = jnp.concatenate([feature_grad, next_rows], axis=1)
    stream_grad = conv_taps[:, 0, None, :] * grad_padded[:, 0:tok_rows, :]
    for offset in range(1, tap_count):
        stream_grad = (
            stream_grad
            + conv_taps[:, offset, None, :] * grad_padded[:, offset : offset + tok_rows, :]
        )
    input_grad = stream_grad.astype(jnp.bfloat16)[None]
    taps_grad = jnp.stack(
        [
            jnp.sum(
                feature_grad * padded[:, edge_rows - offset : edge_rows - offset + tok_rows, :],
                axis=1,
            )
            for offset in range(tap_count)
        ],
        axis=1,
    )
    skip_grad = jnp.sum(grad_z * drive, axis=0)
    residue_grad = coeff_grad * root_norm
    rate_grad = -decays * decay_grad + coeff_grad * residues * decays * decays / root_norm
    grad_sums = lax.psum((taps_grad, residue_grad, rate_grad, skip_grad), ("dp", "ctx"))
    totals = lax.psum(tuple((jnp.sum(member * member) for member in grad_sums)), "tp")
    full_width = width * lax.axis_size("tp")
    entries = (3 * tap_count * full_width, order * full_width, order * full_width, full_width)
    updates = [
        member / jnp.maximum(1.0, jnp.sqrt(total / entry_count))
        for member, total, entry_count in zip(grad_sums, totals, entries)
    ]
    return (mixed, input_grad, updates[0], updates[1], updates[2], updates[3])


LANES = 128
SUBL = 8
HALO = 8
GROUP = 4
MESH = pl.DeviceIdType.MESH
F32 = jnp.float32


def iota_rows():
    return lax.broadcasted_iota(jnp.int32, (SUBL, LANES), 0)


def mega(sizes, x, cot, taps, res, rate, skip, norm, mixed, ig, upd,
         prev, nxt, nct, xs, ct, feat, drive, gz, pre_f, pre_b, sum_f, sum_b, got_f, got_b,
         tab, in_f, in_b, lt, at, hist, acc_c, acc_d, ms, fg, grads, rs, ag, tot, tot_tp, tot_all,
         halo_send, halo_recv, f_send, f_recv, b_send, b_recv,
         rs_send, rs_recv, ag_send, ag_recv, tp_send, tp_recv, all_send, all_recv):
    ndp, nctx, ntp, order, tap_count = sizes
    tok, width = cot.shape
    blocks = width // LANES
    group = ndp * nctx
    seg = (tok + HALO) // SUBL
    last = seg - 1 - HALO
    grad_rows = grads.shape[1]
    me_dp = lax.axis_index("dp")
    me = lax.axis_index("ctx")
    me_tp = lax.axis_index("tp")
    me_g = me_dp * nctx + me

    def peer(p):
        return {"dp": p // nctx, "ctx": lax.rem(p, nctx)}

    barrier = pltpu.get_barrier_semaphore()
    for k in range(1, group):
        p = lax.rem(me_g + k, group)
        pl.semaphore_signal(barrier, inc=1, device_id=peer(p), device_id_type=MESH)
    for k in range(1, ntp):
        q = lax.rem(me_tp + k, ntp)
        pl.semaphore_signal(barrier, inc=1, device_id={"tp": q}, device_id_type=MESH)
    pl.semaphore_wait(barrier, group - 1 + ntp - 1)

    def remote(src, dst, send, recv, where):
        return pltpu.make_async_remote_copy(
            src_ref=src, dst_ref=dst, send_sem=send, recv_sem=recv,
            device_id=where, device_id_type=MESH)

    down = remote(x.at[:, pl.ds(tok - HALO, HALO), :], prev, halo_send.at[0], halo_recv.at[0],
                  {"ctx": jnp.minimum(me + 1, nctx - 1)})
    up = remote(x.at[:, pl.ds(0, HALO), :], nxt, halo_send.at[1], halo_recv.at[1],
                {"ctx": jnp.maximum(me - 1, 0)})
    upc = remote(cot.at[pl.ds(0, HALO), :], nct, halo_send.at[2], halo_recv.at[2],
                 {"ctx": jnp.maximum(me - 1, 0)})

    @pl.when(me < nctx - 1)
    def _():
        down.start()

    @pl.when(me > 0)
    def _():
        up.start()
        upc.start()

    @pl.when(me == 0)
    def _():
        prev[...] = jnp.zeros_like(prev)

    @pl.when(me == nctx - 1)
    def _():
        nxt[...] = jnp.zeros_like(nxt)
        nct[...] = jnp.zeros_like(nct)

    @pl.when(me > 0)
    def _():
        down.wait_recv()

    @pl.when(me < nctx - 1)
    def _():
        up.wait_recv()
        upc.wait_recv()

    def lanes(b):
        return pl.ds(pl.multiple_of(b * LANES, LANES), LANES)

    def row(ref, n, b):
        return jnp.broadcast_to(ref[pl.ds(n, 1), lanes(b)], (SUBL, LANES))

    def trow(k, b, n):
        return jnp.broadcast_to(tab[k, b, pl.ds(n, 1), :], (SUBL, LANES))

    def at_j(j):
        return pl.ds(j * SUBL, SUBL)

    def strided(j):
        return pl.ds(j, SUBL, stride=seg)

    def f_copy(b, far):
        return remote(sum_f.at[b], got_f.at[far - 1, b], f_send.at[far - 1, b], f_recv.at[far - 1, b],
                      {"ctx": jnp.minimum(me + far, nctx - 1)})

    def b_copy(b, far):
        return remote(sum_b.at[b], got_b.at[far - 1, b], b_send.at[far - 1, b], b_recv.at[far - 1, b],
                      {"ctx": jnp.maximum(me - far, 0)})

    def first(i, carry):
        b = lax.rem(me_g + 1 + i, blocks)
        lo = lanes(b)
        rates = rate[:, lo]
        tab[0, b] = jnp.exp(-rates)
        tab[1, b] = jnp.exp(-rates * seg)
        tab[2, b] = jnp.exp(-rates * (2 * seg))
        tab[3, b] = jnp.exp(-rates * (4 * seg))
        tab[4, b] = jnp.exp(-rates * (seg - HALO))
        root = norm[:, lo]
        tab[5, b] = root
        tab[6, b] = res[:, lo] * root
        tab[7, b] = rates
        for s in range(3):
            xs[b, s, 0:HALO, :] = prev[s, :, lo].astype(F32)
            xs[b, s, tok + HALO : tok + 2 * HALO, :] = nxt[s, :, lo].astype(F32)
            for r in range(tok // 16):
                xs[b, s, HALO + 16 * r : HALO + 16 * r + 16, :] = x[s, 16 * r : 16 * r + 16, lo].astype(F32)
        ct[b, tok : tok + HALO, :] = nct[:, lo].astype(F32)
        for r in range(tok // 16):
            ct[b, 16 * r : 16 * r + 16, :] = cot[16 * r : 16 * r + 16, lo].astype(F32)
        for s in range(3):
            w = [row(taps, s * tap_count + o, b) for o in range(tap_count)]
            for j in range(seg):
                total = w[0] * xs[b, s, strided(HALO + j), :]
                for o in range(1, tap_count):
                    total = total + w[o] * xs[b, s, strided(HALO + j - o), :]
                feat[b, s, at_j(j), :] = total
                if s == 0:
                    gz[b, at_j(j), :] = total * ct[b, strided(j), :]
                if s == 2:
                    drive[b, at_j(j), :] = total * feat[b, 1, at_j(j), :]
        rows_at = iota_rows()

        def modes(g, c):
            ns = [g * GROUP + m for m in range(GROUP)]
            d = [trow(0, b, n) for n in ns]
            s = [drive[b, at_j(0), :]] * GROUP
            a = [gz[b, at_j(seg - 1), :]] * GROUP
            mid_s = s if last == 0 else None
            mid_a = a if seg - 1 == HALO else None
            for j in range(1, seg):
                dr = drive[b, at_j(j), :]
                gr = gz[b, at_j(seg - 1 - j), :]
                s = [d[m] * s[m] + dr for m in range(GROUP)]
                a = [d[m] * a[m] + gr for m in range(GROUP)]
                if j == last:
                    mid_s = s
                if seg - 1 - j == HALO:
                    mid_a = a
            for m, n in enumerate(ns):
                y, z = s[m], a[m]
                for k, far in ((1, 1), (2, 2), (3, 4)):
                    p = trow(k, b, n)
                    y = y + jnp.where(rows_at >= far, p * pltpu.roll(y, far, 0), 0.0)
                    z = z + jnp.where(rows_at < SUBL - far, p * pltpu.roll(z, SUBL - far, 0), 0.0)
                y = jnp.where(rows_at >= 1, pltpu.roll(y, 1, 0), 0.0)
                z = jnp.where(rows_at < SUBL - 1, pltpu.roll(z, SUBL - 1, 0), 0.0)
                pre_f[b, n] = y
                pre_b[b, n] = z
                p = trow(4, b, n)
                sum_f[b, pl.ds(n, 1), :] = (mid_s[m] + p * y)[SUBL - 1 : SUBL, :]
                sum_b[b, pl.ds(n, 1), :] = (mid_a[m] + p * z)[0:1, :]
            return c

        lax.fori_loop(0, order // GROUP, modes, 0)
        for far in range(1, nctx):
            @pl.when(me + far < nctx)
            def _():
                f_copy(b, far).start()

            @pl.when(me >= far)
            def _():
                b_copy(b, far).start()
        return carry

    lax.fori_loop(0, blocks, first, 0)

    def rs_copy(b):
        return remote(grads.at[b], rs.at[me_g], rs_send.at[b], rs_recv.at[me_g], peer(b))

    def second(i, carry):
        b = lax.rem(me_g + 1 + i, blocks)
        lo = lanes(b)
        rates = rate[:, lo]
        in_f[...] = jnp.zeros_like(in_f)
        in_b[...] = jnp.zeros_like(in_b)
        for far in range(1, nctx):
            scale = jnp.exp(-rates * (tok * (far - 1)))

            @pl.when(me >= far)
            def _():
                f_copy(b, far).wait_recv()
                in_f[...] += scale * got_f[far - 1, b]

            @pl.when(me + far < nctx)
            def _():
                b_copy(b, far).wait_recv()
                in_b[...] += scale * got_b[far - 1, b]
        lt[...] = jnp.zeros_like(lt)
        at[...] = jnp.zeros_like(at)
        rows_at = iota_rows()
        seg_f = rows_at.astype(F32) * (-float(seg))
        seg_b = (SUBL - 1 - rows_at).astype(F32) * (-float(seg))
        zero = jnp.zeros((SUBL, LANES), F32)

        def fold(head, rest):
            return jnp.sum(head + jnp.where(rows_at < SUBL - 1, rest, 0.0), axis=0, keepdims=True)

        def modes(g, carried):
            ns = [g * GROUP + m for m in range(GROUP)]
            d = [trow(0, b, n) for n in ns]
            c = [trow(6, b, n) for n in ns]
            rr = [trow(7, b, n) for n in ns]
            s = [pre_f[b, n] + jnp.exp(seg_f * rr[m]) * jnp.broadcast_to(in_f[pl.ds(n, 1), :], (SUBL, LANES))
                 for m, n in enumerate(ns)]
            a = [pre_b[b, n] + jnp.exp(seg_b * rr[m]) * jnp.broadcast_to(in_b[pl.ds(n, 1), :], (SUBL, LANES))
                 for m, n in enumerate(ns)]
            head, rest = [zero] * GROUP, [zero] * GROUP
            for j in range(seg):
                dr = drive[b, at_j(j), :]
                gr = gz[b, at_j(j), :]
                for m in range(GROUP):
                    hist[m, j] = s[m]
                s = [d[m] * s[m] + dr for m in range(GROUP)]
                out = lt[at_j(j), :]
                for m in range(GROUP):
                    out = out + c[m] * s[m]
                lt[at_j(j), :] = out
                if j <= last:
                    head = [head[m] + gr * s[m] for m in range(GROUP)]
                else:
                    rest = [rest[m] + gr * s[m] for m in range(GROUP)]
            for m, n in enumerate(ns):
                acc_c[pl.ds(n, 1), :] = fold(head[m], rest[m])
            head, rest = [zero] * GROUP, [zero] * GROUP
            for j in reversed(range(seg)):
                gr = gz[b, at_j(j), :]
                a = [d[m] * a[m] + gr for m in range(GROUP)]
                out = at[at_j(j), :]
                for m in range(GROUP):
                    out = out + c[m] * a[m]
                at[at_j(j), :] = out
                if j <= last:
                    head = [head[m] + a[m] * hist[m, j] for m in range(GROUP)]
                else:
                    rest = [rest[m] + a[m] * hist[m, j] for m in range(GROUP)]
            for m, n in enumerate(ns):
                acc_d[pl.ds(n, 1), :] = fold(head[m], rest[m])
            return carried

        lax.fori_loop(0, order // GROUP, modes, 0)
        decays, root, coeffs = tab[0, b], tab[5, b], tab[6, b]
        coeff_grad = acc_c[...]
        grads[b, 0:order, :] = coeff_grad * root
        grads[b, order : 2 * order, :] = (
            -decays * (coeffs * acc_d[...]) + coeff_grad * res[:, lo] * decays * decays / root)
        gain = row(skip, 0, b)
        head, rest = zero, zero
        for j in range(seg):
            dr = drive[b, at_j(j), :]
            gr = gz[b, at_j(j), :]
            mixer = lt[at_j(j), :] + gain * dr
            ms[strided(j), :] = feat[b, 0, at_j(j), :] * mixer
            fg[0, strided(j), :] = ct[b, strided(j), :] * mixer
            grad_drive = at[at_j(j), :] + gain * gr
            fg[1, strided(j), :] = grad_drive * feat[b, 2, at_j(j), :]
            fg[2, strided(j), :] = grad_drive * feat[b, 1, at_j(j), :]
            if j <= last:
                head = head + gr * dr
            else:
                rest = rest + gr * dr
        base = 2 * order
        grads[b, base + 3 * tap_count : base + 3 * tap_count + 1, :] = fold(head, rest)
        pad = grad_rows - (base + 3 * tap_count + 1)
        grads[b, base + 3 * tap_count + 1 : grad_rows, :] = jnp.zeros((pad, LANES), F32)
        for r in range(tok // 16):
            mixed[16 * r : 16 * r + 16, lo] = ms[16 * r : 16 * r + 16, :].astype(mixed.dtype)
        for s in range(3):
            w = [row(taps, s * tap_count + o, b) for o in range(tap_count)]
            sums = [zero] * tap_count
            for r in range(tok // 16):
                parts = []
                for half in range(2):
                    at_row = 16 * r + 8 * half
                    here = fg[s, at_row : at_row + SUBL, :]
                    total = w[0] * here
                    sums[0] = sums[0] + here * xs[b, s, HALO + at_row : HALO + at_row + SUBL, :]
                    for o in range(1, tap_count):
                        total = total + w[o] * fg[s, at_row + o : at_row + o + SUBL, :]
                        sums[o] = sums[o] + here * xs[b, s, HALO + at_row - o : HALO + at_row - o + SUBL, :]
                    parts.append(total)
                ig[s, 16 * r : 16 * r + 16, lo] = jnp.concatenate(parts, axis=0).astype(ig.dtype)
            for o in range(tap_count):
                at_out = base + s * tap_count + o
                grads[b, at_out : at_out + 1, :] = jnp.sum(sums[o], axis=0, keepdims=True)

        @pl.when(b != me_g)
        def _():
            rs_copy(b).start()

        return carry

    lax.fori_loop(0, blocks, second, 0)

    others = [lax.rem(me_g + k, group) for k in range(1, group)]
    total = grads[me_g]
    for p in others:
        remote(grads.at[p], rs.at[p], rs_send.at[p], rs_recv.at[p], peer(p)).wait_recv()
        total = total + rs[p]
    ag[me_g] = total
    for p in others:
        remote(ag.at[me_g], ag.at[me_g], ag_send.at[p], ag_recv.at[me_g], peer(p)).start()
    square = total * total
    res_sq = jnp.sum(square[0:order, :], axis=0, keepdims=True)
    rate_sq = jnp.sum(square[order : 2 * order, :], axis=0, keepdims=True)
    skip_at = 2 * order + 3 * tap_count
    skip_sq = square[skip_at : skip_at + 1, :]
    rest_sq = jnp.sum(
        jnp.where(lax.broadcasted_iota(jnp.int32, (grad_rows - 2 * order, LANES), 0) < 3 * tap_count,
                  square[2 * order :, :], 0.0), axis=0, keepdims=True)
    rows_at = iota_rows()
    tile = jnp.where(rows_at == 0, res_sq, jnp.where(rows_at == 1, rate_sq,
                     jnp.where(rows_at == 2, rest_sq, jnp.where(rows_at == 3, skip_sq, 0.0))))
    tot[...] = tile
    tps = [lax.rem(me_tp + k, ntp) for k in range(1, ntp)]
    for q in tps:
        remote(tot, tot_tp.at[me_tp], tp_send.at[q], tp_recv.at[me_tp], {"tp": q}).start()
    for q in tps:
        remote(tot, tot_tp.at[q], tp_send.at[q], tp_recv.at[q], {"tp": q}).wait_recv()
        tile = tile + tot_tp[q]
    tot_all[me_g] = tile
    for p in others:
        remote(tot_all.at[me_g], tot_all.at[me_g], all_send.at[p], all_recv.at[me_g], peer(p)).start()
    for p in others:
        remote(tot_all.at[p], tot_all.at[p], all_send.at[p], all_recv.at[p], peer(p)).wait_recv()
        tile = tile + tot_all[p]
    sums = jnp.sum(tile, axis=1, keepdims=True)
    full = width * ntp
    counts = (order * full, order * full, 3 * tap_count * full, full)
    scales = [1.0 / jnp.maximum(1.0, jnp.sqrt(sums[k : k + 1, :] * (1.0 / counts[k]))) for k in range(4)]
    which = lax.broadcasted_iota(jnp.int32, (grad_rows, 1), 0)
    scale = jnp.where(which < order, scales[0], jnp.where(which < 2 * order, scales[1],
                      jnp.where(which < skip_at, scales[2], scales[3])))
    scale = jnp.broadcast_to(scale, (grad_rows, LANES))
    upd[:, lanes(me_g)] = ag[me_g] * scale
    for p in others:
        remote(ag.at[p], ag.at[p], ag_send.at[p], ag_recv.at[p], peer(p)).wait_recv()
        upd[:, lanes(p)] = ag[p] * scale

    @pl.when(me < nctx - 1)
    def _():
        down.wait_send()

    @pl.when(me > 0)
    def _():
        up.wait_send()
        upc.wait_send()

    def drain(b, carry):
        for far in range(1, nctx):
            @pl.when(me + far < nctx)
            def _():
                f_copy(b, far).wait_send()

            @pl.when(me >= far)
            def _():
                b_copy(b, far).wait_send()
        return carry

    lax.fori_loop(0, blocks, drain, 0)
    for p in others:
        rs_copy(p).wait_send()
        remote(ag.at[me_g], ag.at[me_g], ag_send.at[p], ag_recv.at[me_g], peer(p)).wait_send()
        remote(tot_all.at[me_g], tot_all.at[me_g], all_send.at[p], all_recv.at[me_g], peer(p)).wait_send()
    for q in tps:
        remote(tot, tot_tp.at[me_tp], tp_send.at[q], tp_recv.at[me_tp], {"tp": q}).wait_send()


def fused(projected, cotangent, conv_taps, residues, decay_rates, skip_gain):
    ndp, nctx, ntp = (lax.axis_size(a) for a in ("dp", "ctx", "tp"))
    _, _, tok, width = projected.shape
    order = residues.shape[0]
    tap_count = conv_taps.shape[1]
    blocks = width // LANES
    group = ndp * nctx
    seg = (tok + HALO) // SUBL
    grad_rows = -(-(2 * order + 3 * tap_count + 1) // SUBL) * SUBL
    vm = pl.BlockSpec(memory_space=pltpu.VMEM)
    dma = pltpu.SemaphoreType.DMA
    V = pltpu.VMEM
    bf = jnp.bfloat16
    mixed, ig, upd = pl.pallas_call(
        functools.partial(mega, (ndp, nctx, ntp, order, tap_count)),
        out_shape=(
            jax.ShapeDtypeStruct((tok, width), bf),
            jax.ShapeDtypeStruct((3, tok, width), bf),
            jax.ShapeDtypeStruct((grad_rows, width), F32),
        ),
        in_specs=[vm] * 7,
        out_specs=(vm, vm, vm),
        scratch_shapes=[
            V((3, HALO, width), bf), V((3, HALO, width), bf), V((HALO, width), bf),
            V((blocks, 3, tok + 2 * HALO, LANES), F32), V((blocks, tok + HALO, LANES), F32),
            V((blocks, 3, seg * SUBL, LANES), F32), V((blocks, seg * SUBL, LANES), F32),
            V((blocks, seg * SUBL, LANES), F32),
            V((blocks, order, SUBL, LANES), F32), V((blocks, order, SUBL, LANES), F32),
            V((blocks, order, LANES), F32), V((blocks, order, LANES), F32),
            V((nctx - 1, blocks, order, LANES), F32), V((nctx - 1, blocks, order, LANES), F32),
            V((8, blocks, order, LANES), F32), V((order, LANES), F32), V((order, LANES), F32),
            V((seg * SUBL, LANES), F32), V((seg * SUBL, LANES), F32),
            V((GROUP, seg, SUBL, LANES), F32), V((order, LANES), F32), V((order, LANES), F32),
            V((seg * SUBL, LANES), F32), V((3, seg * SUBL, LANES), F32),
            V((blocks, grad_rows, LANES), F32), V((group, grad_rows, LANES), F32),
            V((group, grad_rows, LANES), F32),
            V((SUBL, LANES), F32), V((ntp, SUBL, LANES), F32), V((group, SUBL, LANES), F32),
            dma((3,)), dma((3,)),
            dma((nctx - 1, blocks)), dma((nctx - 1, blocks)), dma((nctx - 1, blocks)), dma((nctx - 1, blocks)),
            dma((group,)), dma((group,)), dma((group,)), dma((group,)),
            dma((ntp,)), dma((ntp,)), dma((group,)), dma((group,)),
        ],
        compiler_params=pltpu.CompilerParams(
            collective_id=0, has_side_effects=True, vmem_limit_bytes=48 * 1024 * 1024),
    )(projected[0], cotangent[0], conv_taps.reshape(3 * tap_count, width), residues, decay_rates,
      skip_gain.reshape(1, width), jnp.sqrt(-jnp.expm1(-2.0 * decay_rates)))
    base = 2 * order
    return (mixed[None], ig[None],
            upd[base : base + 3 * tap_count].reshape(3, tap_count, width),
            upd[0:order], upd[order:base], upd[base + 3 * tap_count])


def fits(mesh, projected, residues, conv_taps):
    tok = projected.shape[2] // mesh.shape["ctx"]
    width = projected.shape[3] // mesh.shape["tp"]
    group = mesh.shape["dp"] * mesh.shape["ctx"]
    return (width == group * LANES and tok % 16 == 0 and tok >= 64 and mesh.shape["ctx"] > 1
            and mesh.shape["tp"] > 1 and residues.shape[0] % SUBL == 0
            and conv_taps.shape[1] <= HALO - 1 and projected.shape[0] == mesh.shape["dp"])


def solution(mesh):
    in_specs = (
        P("dp", None, "ctx", "tp"),
        P("dp", "ctx", "tp"),
        P(None, None, "tp"),
        P(None, "tp"),
        P(None, "tp"),
        P("tp"),
    )
    out_specs = (
        P("dp", "ctx", "tp"),
        P("dp", None, "ctx", "tp"),
        P(None, None, "tp"),
        P(None, "tp"),
        P(None, "tp"),
        P("tp"),
    )

    def run(projected, cotangent, conv_taps, residues, decay_rates, skip_gain):
        body = fused if fits(mesh, projected, residues, conv_taps) else local
        mapped = jax.shard_map(body, mesh=mesh, in_specs=in_specs, out_specs=out_specs, check_vma=False)
        return mapped(projected, cotangent, conv_taps, residues, decay_rates, skip_gain)

    return run
```

```python
import functools
import jax
import jax.numpy as jnp
from jax import lax
from jax.experimental import pallas as pl
from jax.experimental.pallas import tpu as pltpu
from jax.sharding import PartitionSpec as P


def prefix(x, axis, combine, identity, reverse):
    peers, mine = (lax.axis_size(axis), lax.axis_index(axis))
    everything = jax.tree.map(lambda part: lax.all_gather(part, axis), x)
    start = jax.tree.map(
        lambda part, zero: jnp.broadcast_to(jnp.asarray(zero, part.dtype), part.shape), x, identity
    )

    def step(k, before):
        at = peers - 1 - k if reverse else k
        reached = at > mine if reverse else at < mine
        new = combine(before, jax.tree.map(lambda part: part[at], everything))
        return jax.tree.map(lambda a, b: jnp.where(reached, a, b), new, before)

    return lax.fori_loop(0, peers, step, start)


def shifted(block, axis, distance):
    devices = range(lax.axis_size(axis))
    route = [(i - distance, i) for i in devices if i - distance in devices]
    return lax.ppermute(block, axis, route)


def linear_combine(earlier, later):
    return (earlier[0] * later[0], later[0] * earlier[1] + later[1])


def carry_pass(block_decay, summary, backward):
    identity = (jnp.ones_like(summary), jnp.zeros_like(summary))
    return prefix((block_decay, summary), "ctx", linear_combine, identity, backward)[1]


def local(projected, cotangent, conv_taps, residues, decay_rates, skip_gain):
    streams = projected[0]
    tok_rows = streams.shape[1]
    width = streams.shape[2]
    order = residues.shape[0]
    tap_count = conv_taps.shape[1]
    edge_rows = tap_count - 1
    prev_rows = shifted(streams[:, tok_rows - edge_rows :, :], "ctx", 1)
    padded = jnp.concatenate([prev_rows, streams], axis=1).astype(jnp.float32)
    features = conv_taps[:, 0, None, :] * padded[:, edge_rows : edge_rows + tok_rows, :]
    for offset in range(1, tap_count):
        features = (
            features
            + conv_taps[:, offset, None, :]
            * padded[:, edge_rows - offset : edge_rows - offset + tok_rows, :]
        )
    query = features[0]
    keyed = features[1]
    valued = features[2]
    drive = keyed * valued
    decays = jnp.exp(-decay_rates)
    root_norm = jnp.sqrt(-jnp.expm1(-2.0 * decay_rates))
    coeffs = residues * root_norm
    cot_rows = cotangent[0].astype(jnp.float32)
    grad_z = cot_rows * query
    zeros_state = jnp.zeros((order, width), jnp.float32)

    def local_step(carried, rows):
        state_now, adj_now = carried
        drive_row, grad_row = rows
        state_now = decays * state_now + drive_row[None, :]
        adj_now = decays * adj_now + coeffs * grad_row[None, :]
        return ((state_now, adj_now), None)

    (end_state, first_adjoint), _ = lax.scan(
        local_step, (zeros_state, zeros_state), (drive, grad_z[::-1]), unroll=8
    )
    block_decay = jnp.exp(-decay_rates * tok_rows)
    state_in = carry_pass(block_decay, end_state, False)
    adjoint_in = carry_pass(block_decay, first_adjoint, True)

    def forward_step(carried, rows):
        state_now, coeff_acc = carried
        drive_row, grad_row = rows
        before = state_now
        state_now = decays * state_now + drive_row[None, :]
        coeff_acc = coeff_acc + grad_row[None, :] * state_now
        return ((state_now, coeff_acc), (before, jnp.sum(coeffs * state_now, axis=0)))

    (_, coeff_grad), (state_prev, long_term) = lax.scan(
        forward_step, (state_in, zeros_state), (drive, grad_z), unroll=8
    )

    def backward_step(carried, rows):
        adj_now, decay_acc = carried
        grad_row, before = rows
        adj_now = decays * adj_now + coeffs * grad_row[None, :]
        decay_acc = decay_acc + adj_now * before
        return ((adj_now, decay_acc), jnp.sum(adj_now, axis=0))

    (_, decay_grad), adjoint_total = lax.scan(
        backward_step, (adjoint_in, zeros_state), (grad_z, state_prev), reverse=True, unroll=8
    )
    mixer_out = long_term + skip_gain * drive
    mixed = (query * mixer_out).astype(jnp.bfloat16)[None]
    grad_drive = adjoint_total + skip_gain * grad_z
    feature_grad = jnp.stack(
        [cot_rows * mixer_out, grad_drive * valued, grad_drive * keyed], axis=0
    )
    next_rows = shifted(feature_grad[:, :edge_rows, :], "ctx", -1)
    grad_padded = jnp.concatenate([feature_grad, next_rows], axis=1)
    stream_grad = conv_taps[:, 0, None, :] * grad_padded[:, 0:tok_rows, :]
    for offset in range(1, tap_count):
        stream_grad = (
            stream_grad
            + conv_taps[:, offset, None, :] * grad_padded[:, offset : offset + tok_rows, :]
        )
    input_grad = stream_grad.astype(jnp.bfloat16)[None]
    taps_grad = jnp.stack(
        [
            jnp.sum(
                feature_grad * padded[:, edge_rows - offset : edge_rows - offset + tok_rows, :],
                axis=1,
            )
            for offset in range(tap_count)
        ],
        axis=1,
    )
    skip_grad = jnp.sum(grad_z * drive, axis=0)
    residue_grad = coeff_grad * root_norm
    rate_grad = -decays * decay_grad + coeff_grad * residues * decays * decays / root_norm
    grad_sums = lax.psum((taps_grad, residue_grad, rate_grad, skip_grad), ("dp", "ctx"))
    totals = lax.psum(tuple((jnp.sum(member * member) for member in grad_sums)), "tp")
    full_width = width * lax.axis_size("tp")
    entries = (3 * tap_count * full_width, order * full_width, order * full_width, full_width)
    updates = [
        member / jnp.maximum(1.0, jnp.sqrt(total / entry_count))
        for member, total, entry_count in zip(grad_sums, totals, entries)
    ]
    return (mixed, input_grad, updates[0], updates[1], updates[2], updates[3])


LANES = 128
SUBL = 8
HALO = 8
GROUP = 4
GRANT = 62 * 1024 * 1024
MESH = pl.DeviceIdType.MESH
F32 = jnp.float32


def iota_rows():
    return lax.broadcasted_iota(jnp.int32, (SUBL, LANES), 0)


def mega(sizes, x_hbm, cot_hbm, taps_hbm, res_hbm, rate_hbm, skip_hbm,
         mixed, ig, taps_upd, res_upd, rate_upd, skip_upd,
         x, cot, taps, res, rate, skip, load_sem, prev, nxt, nct, xs, ct, feat, drive, gz, pre_f, pre_b, sum_f, sum_b, got_f, got_b,
         tab, in_f, in_b, lt, at, hist, acc_c, acc_d, ms, fg, grads, rs, ag, tot, tot_tp, tot_all,
         halo_send, halo_recv, f_send, f_recv, b_send, b_recv,
         rs_send, rs_recv, ag_send, ag_recv, tp_send, tp_recv, all_send, all_recv):
    ndp, nctx, ntp, order, tap_count = sizes
    tok, width = cot.shape
    blocks = width // LANES
    group = ndp * nctx
    seg = (tok + HALO) // SUBL
    last = seg - 1 - HALO
    grad_rows = grads.shape[1]
    me_dp = lax.axis_index("dp")
    me = lax.axis_index("ctx")
    me_tp = lax.axis_index("tp")
    me_g = me_dp * nctx + me

    def peer(p):
        return {"dp": p // nctx, "ctx": lax.rem(p, nctx)}

    pairs = ((rate_hbm, rate), (x_hbm, x), (cot_hbm, cot), (res_hbm, res), (taps_hbm, taps), (skip_hbm, skip))
    loads = [pltpu.make_async_copy(src, dst, load_sem.at[k]) for k, (src, dst) in enumerate(pairs)]
    for load in loads:
        load.start()
    barrier = pltpu.get_barrier_semaphore()
    for k in range(1, group):
        p = lax.rem(me_g + k, group)
        pl.semaphore_signal(barrier, inc=1, device_id=peer(p), device_id_type=MESH)
    for k in range(1, ntp):
        q = lax.rem(me_tp + k, ntp)
        pl.semaphore_signal(barrier, inc=1, device_id={"tp": q}, device_id_type=MESH)
    def lanes(b):
        return pl.ds(pl.multiple_of(b * LANES, LANES), LANES)

    def row(ref, n, b):
        return jnp.broadcast_to(ref[pl.ds(n, 1), lanes(b)], (SUBL, LANES))

    def trow(k, b, n):
        return jnp.broadcast_to(tab[k, b, pl.ds(n, 1), :], (SUBL, LANES))

    def at_j(j):
        return pl.ds(j * SUBL, SUBL)

    def strided(j):
        return pl.ds(j, SUBL, stride=seg)

    def turn(i):
        return lax.rem(i + me_dp * (blocks // ndp), blocks)

    for load in loads:
        load.wait()

    def fill(b, carry):
        lo = lanes(b)
        rates = rate[:, lo]
        tab[0, b] = jnp.exp(-rates)
        tab[1, b] = jnp.exp(-rates * seg)
        tab[2, b] = jnp.exp(-rates * (2 * seg))
        tab[3, b] = jnp.exp(-rates * (4 * seg))
        tab[4, b] = jnp.exp(-rates * (seg - HALO))
        twice = 2.0 * rates
        series = jnp.ones_like(twice)
        for k in range(12, 1, -1):
            series = 1.0 - twice * series * (1.0 / k)
        root = jnp.sqrt(jnp.where(twice < 0.5, twice * series, 1.0 - jnp.exp(-twice)))
        tab[5, b] = root
        tab[6, b] = res[:, lo] * root
        tab[7, b] = rates
        for s in range(3):
            for r in range(tok // 16):
                xs[b, s, HALO + 16 * r : HALO + 16 * r + 16, :] = x[s, 16 * r : 16 * r + 16, lo].astype(F32)
        for r in range(tok // 16):
            ct[b, 16 * r : 16 * r + 16, :] = cot[16 * r : 16 * r + 16, lo].astype(F32)
        return carry

    lax.fori_loop(0, blocks // 2, fill, 0)
    pl.semaphore_wait(barrier, group - 1 + ntp - 1)

    def remote(src, dst, send, recv, where):
        return pltpu.make_async_remote_copy(
            src_ref=src, dst_ref=dst, send_sem=send, recv_sem=recv,
            device_id=where, device_id_type=MESH)

    down = remote(x_hbm.at[:, pl.ds(tok - HALO, HALO), :], prev, halo_send.at[0], halo_recv.at[0],
                  {"ctx": jnp.minimum(me + 1, nctx - 1)})
    up = remote(x_hbm.at[:, pl.ds(0, HALO), :], nxt, halo_send.at[1], halo_recv.at[1],
                {"ctx": jnp.maximum(me - 1, 0)})
    upc = remote(cot_hbm.at[pl.ds(0, HALO), :], nct, halo_send.at[2], halo_recv.at[2],
                 {"ctx": jnp.maximum(me - 1, 0)})

    @pl.when(me < nctx - 1)
    def _():
        down.start()

    @pl.when(me > 0)
    def _():
        up.start()
        upc.start()

    @pl.when(me == 0)
    def _():
        prev[...] = jnp.zeros_like(prev)

    @pl.when(me == nctx - 1)
    def _():
        nxt[...] = jnp.zeros_like(nxt)
        nct[...] = jnp.zeros_like(nct)

    lax.fori_loop(blocks // 2, blocks, fill, 0)

    @pl.when(me > 0)
    def _():
        down.wait_recv()

    @pl.when(me < nctx - 1)
    def _():
        up.wait_recv()
        upc.wait_recv()

    def f_copy(b, far):
        return remote(sum_f.at[b], got_f.at[far - 1, b], f_send.at[far - 1, b], f_recv.at[far - 1, b],
                      {"ctx": jnp.minimum(me + far, nctx - 1)})

    def b_copy(b, far):
        return remote(sum_b.at[b], got_b.at[far - 1, b], b_send.at[far - 1, b], b_recv.at[far - 1, b],
                      {"ctx": jnp.maximum(me - far, 0)})

    def first(i, carry):
        b = turn(i)
        lo = lanes(b)
        for s in range(3):
            xs[b, s, 0:HALO, :] = prev[s, :, lo].astype(F32)
            xs[b, s, tok + HALO : tok + 2 * HALO, :] = nxt[s, :, lo].astype(F32)
        ct[b, tok : tok + HALO, :] = nct[:, lo].astype(F32)
        for s in range(3):
            w = [jnp.broadcast_to(taps[s, o : o + 1, lo], (SUBL, LANES)) for o in range(tap_count)]
            for j in range(seg):
                total = w[0] * xs[b, s, strided(HALO + j), :]
                for o in range(1, tap_count):
                    total = total + w[o] * xs[b, s, strided(HALO + j - o), :]
                feat[b, s, at_j(j), :] = total
                if s == 0:
                    gz[b, at_j(j), :] = total * ct[b, strided(j), :]
                if s == 2:
                    drive[b, at_j(j), :] = total * feat[b, 1, at_j(j), :]
        rows_at = iota_rows()

        def modes(g, c):
            ns = [g * GROUP + m for m in range(GROUP)]
            d = [trow(0, b, n) for n in ns]
            s = [drive[b, at_j(0), :]] * GROUP
            a = [gz[b, at_j(seg - 1), :]] * GROUP
            mid_s = s if last == 0 else None
            mid_a = a if seg - 1 == HALO else None
            for j in range(1, seg):
                dr = drive[b, at_j(j), :]
                gr = gz[b, at_j(seg - 1 - j), :]
                s = [d[m] * s[m] + dr for m in range(GROUP)]
                a = [d[m] * a[m] + gr for m in range(GROUP)]
                if j == last:
                    mid_s = s
                if seg - 1 - j == HALO:
                    mid_a = a
            for m, n in enumerate(ns):
                y, z = s[m], a[m]
                for k, far in ((1, 1), (2, 2), (3, 4)):
                    p = trow(k, b, n)
                    y = y + jnp.where(rows_at >= far, p * pltpu.roll(y, far, 0), 0.0)
                    z = z + jnp.where(rows_at < SUBL - far, p * pltpu.roll(z, SUBL - far, 0), 0.0)
                y = jnp.where(rows_at >= 1, pltpu.roll(y, 1, 0), 0.0)
                z = jnp.where(rows_at < SUBL - 1, pltpu.roll(z, SUBL - 1, 0), 0.0)
                pre_f[b, n] = y
                pre_b[b, n] = z
                p = trow(4, b, n)
                sum_f[b, pl.ds(n, 1), :] = (mid_s[m] + p * y)[SUBL - 1 : SUBL, :]
                sum_b[b, pl.ds(n, 1), :] = (mid_a[m] + p * z)[0:1, :]
            return c

        lax.fori_loop(0, order // GROUP, modes, 0)
        for far in range(1, nctx):
            @pl.when(me + far < nctx)
            def _():
                f_copy(b, far).start()

            @pl.when(me >= far)
            def _():
                b_copy(b, far).start()
        return carry

    lax.fori_loop(0, blocks, first, 0)

    def rs_copy(b):
        return remote(grads.at[b], rs.at[me_g], rs_send.at[b], rs_recv.at[me_g], peer(b))

    def second(i, carry):
        b = turn(i)
        lo = lanes(b)
        rates = rate[:, lo]
        in_f[...] = jnp.zeros_like(in_f)
        in_b[...] = jnp.zeros_like(in_b)
        for far in range(1, nctx):
            scale = jnp.exp(-rates * (tok * (far - 1)))

            @pl.when(me >= far)
            def _():
                f_copy(b, far).wait_recv()
                in_f[...] += scale * got_f[far - 1, b]

            @pl.when(me + far < nctx)
            def _():
                b_copy(b, far).wait_recv()
                in_b[...] += scale * got_b[far - 1, b]
        lt[...] = jnp.zeros_like(lt)
        at[...] = jnp.zeros_like(at)
        rows_at = iota_rows()
        seg_f = rows_at.astype(F32) * (-float(seg))
        seg_b = (SUBL - 1 - rows_at).astype(F32) * (-float(seg))
        zero = jnp.zeros((SUBL, LANES), F32)

        def fold(head, rest):
            return jnp.sum(head + jnp.where(rows_at < SUBL - 1, rest, 0.0), axis=0, keepdims=True)

        def modes(g, carried):
            ns = [g * GROUP + m for m in range(GROUP)]
            d = [trow(0, b, n) for n in ns]
            c = [trow(6, b, n) for n in ns]
            rr = [trow(7, b, n) for n in ns]
            s = [pre_f[b, n] + jnp.exp(seg_f * rr[m]) * jnp.broadcast_to(in_f[pl.ds(n, 1), :], (SUBL, LANES))
                 for m, n in enumerate(ns)]
            a = [pre_b[b, n] + jnp.exp(seg_b * rr[m]) * jnp.broadcast_to(in_b[pl.ds(n, 1), :], (SUBL, LANES))
                 for m, n in enumerate(ns)]
            head, rest = [zero] * GROUP, [zero] * GROUP
            for j in range(seg):
                dr = drive[b, at_j(j), :]
                gr = gz[b, at_j(j), :]
                for m in range(GROUP):
                    hist[m, j] = s[m]
                s = [d[m] * s[m] + dr for m in range(GROUP)]
                out = lt[at_j(j), :]
                for m in range(GROUP):
                    out = out + c[m] * s[m]
                lt[at_j(j), :] = out
                if j <= last:
                    head = [head[m] + gr * s[m] for m in range(GROUP)]
                else:
                    rest = [rest[m] + gr * s[m] for m in range(GROUP)]
            for m, n in enumerate(ns):
                acc_c[pl.ds(n, 1), :] = fold(head[m], rest[m])
            head, rest = [zero] * GROUP, [zero] * GROUP
            for j in reversed(range(seg)):
                gr = gz[b, at_j(j), :]
                a = [d[m] * a[m] + gr for m in range(GROUP)]
                out = at[at_j(j), :]
                for m in range(GROUP):
                    out = out + c[m] * a[m]
                at[at_j(j), :] = out
                if j <= last:
                    head = [head[m] + a[m] * hist[m, j] for m in range(GROUP)]
                else:
                    rest = [rest[m] + a[m] * hist[m, j] for m in range(GROUP)]
            for m, n in enumerate(ns):
                acc_d[pl.ds(n, 1), :] = fold(head[m], rest[m])
            return carried

        lax.fori_loop(0, order // GROUP, modes, 0)
        decays, root, coeffs = tab[0, b], tab[5, b], tab[6, b]
        coeff_grad = acc_c[...]
        grads[b, 0:order, :] = coeff_grad * root
        grads[b, order : 2 * order, :] = (
            -decays * (coeffs * acc_d[...]) + coeff_grad * res[:, lo] * decays * decays / root)
        gain = row(skip, 0, b)
        head, rest = zero, zero
        for j in range(seg):
            dr = drive[b, at_j(j), :]
            gr = gz[b, at_j(j), :]
            mixer = lt[at_j(j), :] + gain * dr
            ms[strided(j), :] = feat[b, 0, at_j(j), :] * mixer
            fg[0, strided(j), :] = ct[b, strided(j), :] * mixer
            grad_drive = at[at_j(j), :] + gain * gr
            fg[1, strided(j), :] = grad_drive * feat[b, 2, at_j(j), :]
            fg[2, strided(j), :] = grad_drive * feat[b, 1, at_j(j), :]
            if j <= last:
                head = head + gr * dr
            else:
                rest = rest + gr * dr
        base = 2 * order
        grads[b, base + 3 * tap_count : base + 3 * tap_count + 1, :] = fold(head, rest)
        pad = grad_rows - (base + 3 * tap_count + 1)
        grads[b, base + 3 * tap_count + 1 : grad_rows, :] = jnp.zeros((pad, LANES), F32)
        for r in range(tok // 16):
            mixed[16 * r : 16 * r + 16, lo] = ms[16 * r : 16 * r + 16, :].astype(mixed.dtype)
        for s in range(3):
            w = [jnp.broadcast_to(taps[s, o : o + 1, lo], (SUBL, LANES)) for o in range(tap_count)]
            sums = [zero] * tap_count
            for r in range(tok // 16):
                parts = []
                for half in range(2):
                    at_row = 16 * r + 8 * half
                    here = fg[s, at_row : at_row + SUBL, :]
                    total = w[0] * here
                    sums[0] = sums[0] + here * xs[b, s, HALO + at_row : HALO + at_row + SUBL, :]
                    for o in range(1, tap_count):
                        total = total + w[o] * fg[s, at_row + o : at_row + o + SUBL, :]
                        sums[o] = sums[o] + here * xs[b, s, HALO + at_row - o : HALO + at_row - o + SUBL, :]
                    parts.append(total)
                ig[s, 16 * r : 16 * r + 16, lo] = jnp.concatenate(parts, axis=0).astype(ig.dtype)
            for o in range(tap_count):
                at_out = base + s * tap_count + o
                grads[b, at_out : at_out + 1, :] = jnp.sum(sums[o], axis=0, keepdims=True)

        @pl.when(b != me_g)
        def _():
            rs_copy(b).start()

        return carry

    lax.fori_loop(0, blocks, second, 0)

    others = [lax.rem(me_g + k, group) for k in range(1, group)]
    total = grads[me_g]
    for p in others:
        remote(grads.at[p], rs.at[p], rs_send.at[p], rs_recv.at[p], peer(p)).wait_recv()
        total = total + rs[p]
    ag[me_g] = total
    for p in others:
        remote(ag.at[me_g], ag.at[me_g], ag_send.at[p], ag_recv.at[me_g], peer(p)).start()
    square = total * total
    res_sq = jnp.sum(square[0:order, :], axis=0, keepdims=True)
    rate_sq = jnp.sum(square[order : 2 * order, :], axis=0, keepdims=True)
    skip_at = 2 * order + 3 * tap_count
    skip_sq = square[skip_at : skip_at + 1, :]
    rest_sq = jnp.sum(
        jnp.where(lax.broadcasted_iota(jnp.int32, (grad_rows - 2 * order, LANES), 0) < 3 * tap_count,
                  square[2 * order :, :], 0.0), axis=0, keepdims=True)
    rows_at = iota_rows()
    tile = jnp.where(rows_at == 0, res_sq, jnp.where(rows_at == 1, rate_sq,
                     jnp.where(rows_at == 2, rest_sq, jnp.where(rows_at == 3, skip_sq, 0.0))))
    tot[...] = tile
    tps = [lax.rem(me_tp + k, ntp) for k in range(1, ntp)]
    for q in tps:
        remote(tot, tot_tp.at[me_tp], tp_send.at[q], tp_recv.at[me_tp], {"tp": q}).start()
    for q in tps:
        remote(tot, tot_tp.at[q], tp_send.at[q], tp_recv.at[q], {"tp": q}).wait_recv()
        tile = tile + tot_tp[q]
    tot_all[me_g] = tile
    for p in others:
        remote(tot_all.at[me_g], tot_all.at[me_g], all_send.at[p], all_recv.at[me_g], peer(p)).start()
    for p in others:
        remote(tot_all.at[p], tot_all.at[p], all_send.at[p], all_recv.at[p], peer(p)).wait_recv()
        tile = tile + tot_all[p]
    sums = jnp.sum(tile, axis=1, keepdims=True)
    full = width * ntp
    counts = (order * full, order * full, 3 * tap_count * full, full)
    scales = [1.0 / jnp.maximum(1.0, jnp.sqrt(sums[k : k + 1, :] * (1.0 / counts[k]))) for k in range(4)]
    which = lax.broadcasted_iota(jnp.int32, (grad_rows, 1), 0)
    scale = jnp.where(which < order, scales[0], jnp.where(which < 2 * order, scales[1],
                      jnp.where(which < skip_at, scales[2], scales[3])))
    scale = jnp.broadcast_to(scale, (grad_rows, LANES))
    def write(p):
        lo = lanes(p)
        block = ag[p] * scale
        res_upd[:, lo] = block[0:order, :]
        rate_upd[:, lo] = block[order : 2 * order, :]
        for s in range(3):
            at_row = 2 * order + s * tap_count
            taps_upd[s, :, lo] = block[at_row : at_row + tap_count, :]
        skip_upd[:, lo] = block[skip_at : skip_at + 1, :]

    write(me_g)
    for p in others:
        remote(ag.at[p], ag.at[p], ag_send.at[p], ag_recv.at[p], peer(p)).wait_recv()
        write(p)

    @pl.when(me < nctx - 1)
    def _():
        down.wait_send()

    @pl.when(me > 0)
    def _():
        up.wait_send()
        upc.wait_send()

    def drain(b, carry):
        for far in range(1, nctx):
            @pl.when(me + far < nctx)
            def _():
                f_copy(b, far).wait_send()

            @pl.when(me >= far)
            def _():
                b_copy(b, far).wait_send()
        return carry

    lax.fori_loop(0, blocks, drain, 0)
    for p in others:
        rs_copy(p).wait_send()
        remote(ag.at[me_g], ag.at[me_g], ag_send.at[p], ag_recv.at[me_g], peer(p)).wait_send()
        remote(tot_all.at[me_g], tot_all.at[me_g], all_send.at[p], all_recv.at[me_g], peer(p)).wait_send()
    for q in tps:
        remote(tot, tot_tp.at[me_tp], tp_send.at[q], tp_recv.at[me_tp], {"tp": q}).wait_send()


def place(*refs):
    sem = refs[-1]
    copies = [pltpu.make_async_copy(refs[k], refs[6 + k], sem.at[k]) for k in range(6)]
    for copy in copies:
        copy.start()
    for copy in copies:
        copy.wait()


def fused(projected, cotangent, conv_taps, residues, decay_rates, skip_gain):
    ndp, nctx, ntp = (lax.axis_size(a) for a in ("dp", "ctx", "tp"))
    _, _, tok, width = projected.shape
    order = residues.shape[0]
    tap_count = conv_taps.shape[1]
    blocks = width // LANES
    group = ndp * nctx
    seg = (tok + HALO) // SUBL
    grad_rows = -(-(2 * order + 3 * tap_count + 1) // SUBL) * SUBL
    vm = pl.BlockSpec(memory_space=pltpu.VMEM)
    dma = pltpu.SemaphoreType.DMA
    V = pltpu.VMEM
    bf = jnp.bfloat16
    shapes = (
        jax.ShapeDtypeStruct((tok, width), bf),
        jax.ShapeDtypeStruct((3, tok, width), bf),
        jax.ShapeDtypeStruct((3, tap_count, width), F32),
        jax.ShapeDtypeStruct((order, width), F32),
        jax.ShapeDtypeStruct((order, width), F32),
        jax.ShapeDtypeStruct((1, width), F32),
    )
    hbm = pl.BlockSpec(memory_space=pltpu.HBM)
    parts = pl.pallas_call(
        functools.partial(mega, (ndp, nctx, ntp, order, tap_count)),
        out_shape=shapes,
        in_specs=[hbm] * 6,
        out_specs=(vm,) * 6,
        scratch_shapes=[
            V((3, tok, width), bf), V((tok, width), bf), V((3, tap_count, width), F32),
            V((order, width), F32), V((order, width), F32), V((1, width), F32), dma((6,)),
            V((3, HALO, width), bf), V((3, HALO, width), bf), V((HALO, width), bf),
            V((blocks, 3, tok + 2 * HALO, LANES), F32), V((blocks, tok + HALO, LANES), F32),
            V((blocks, 3, seg * SUBL, LANES), F32), V((blocks, seg * SUBL, LANES), F32),
            V((blocks, seg * SUBL, LANES), F32),
            V((blocks, order, SUBL, LANES), F32), V((blocks, order, SUBL, LANES), F32),
            V((blocks, order, LANES), F32), V((blocks, order, LANES), F32),
            V((nctx - 1, blocks, order, LANES), F32), V((nctx - 1, blocks, order, LANES), F32),
            V((8, blocks, order, LANES), F32), V((order, LANES), F32), V((order, LANES), F32),
            V((seg * SUBL, LANES), F32), V((seg * SUBL, LANES), F32),
            V((GROUP, seg, SUBL, LANES), F32), V((order, LANES), F32), V((order, LANES), F32),
            V((seg * SUBL, LANES), F32), V((3, seg * SUBL, LANES), F32),
            V((blocks, grad_rows, LANES), F32), V((group, grad_rows, LANES), F32),
            V((group, grad_rows, LANES), F32),
            V((SUBL, LANES), F32), V((ntp, SUBL, LANES), F32), V((group, SUBL, LANES), F32),
            dma((3,)), dma((3,)),
            dma((nctx - 1, blocks)), dma((nctx - 1, blocks)), dma((nctx - 1, blocks)), dma((nctx - 1, blocks)),
            dma((group,)), dma((group,)), dma((group,)), dma((group,)),
            dma((ntp,)), dma((ntp,)), dma((group,)), dma((group,)),
        ],
        compiler_params=pltpu.CompilerParams(
            collective_id=0, has_side_effects=True, vmem_limit_bytes=GRANT),
    )(projected[0], cotangent[0], conv_taps, residues, decay_rates, skip_gain.reshape(1, width))
    mixed, ig, taps_upd, res_upd, rate_upd, skip_upd = pl.pallas_call(
        place,
        out_shape=shapes,
        in_specs=[vm] * 6,
        out_specs=(hbm,) * 6,
        scratch_shapes=[dma((6,))],
    )(*parts)
    return mixed[None], ig[None], taps_upd, res_upd, rate_upd, skip_upd.reshape(width)


def fits(mesh, projected, residues, conv_taps):
    tok = projected.shape[2] // mesh.shape["ctx"]
    width = projected.shape[3] // mesh.shape["tp"]
    group = mesh.shape["dp"] * mesh.shape["ctx"]
    return (width == group * LANES and tok % 16 == 0 and tok >= 64 and mesh.shape["ctx"] > 1
            and mesh.shape["tp"] > 1 and residues.shape[0] % SUBL == 0
            and conv_taps.shape[1] <= HALO - 1 and projected.shape[0] == mesh.shape["dp"])


def solution(mesh):
    in_specs = (
        P("dp", None, "ctx", "tp"),
        P("dp", "ctx", "tp"),
        P(None, None, "tp"),
        P(None, "tp"),
        P(None, "tp"),
        P("tp"),
    )
    out_specs = (
        P("dp", "ctx", "tp"),
        P("dp", None, "ctx", "tp"),
        P(None, None, "tp"),
        P(None, "tp"),
        P(None, "tp"),
        P("tp"),
    )

    def run(projected, cotangent, conv_taps, residues, decay_rates, skip_gain):
        body = fused if fits(mesh, projected, residues, conv_taps) else local
        mapped = jax.shard_map(body, mesh=mesh, in_specs=in_specs, out_specs=out_specs, check_vma=False)
        return mapped(projected, cotangent, conv_taps, residues, decay_rates, skip_gain)

    return run
```

```python
import functools
import jax
import jax.numpy as jnp
from jax import lax
from jax.experimental import pallas as pl
from jax.experimental.pallas import tpu as pltpu
from jax.sharding import PartitionSpec as P


def prefix(x, axis, combine, identity, reverse):
    peers, mine = (lax.axis_size(axis), lax.axis_index(axis))
    everything = jax.tree.map(lambda part: lax.all_gather(part, axis), x)
    start = jax.tree.map(
        lambda part, zero: jnp.broadcast_to(jnp.asarray(zero, part.dtype), part.shape), x, identity
    )

    def step(k, before):
        at = peers - 1 - k if reverse else k
        reached = at > mine if reverse else at < mine
        new = combine(before, jax.tree.map(lambda part: part[at], everything))
        return jax.tree.map(lambda a, b: jnp.where(reached, a, b), new, before)

    return lax.fori_loop(0, peers, step, start)


def shifted(block, axis, distance):
    devices = range(lax.axis_size(axis))
    route = [(i - distance, i) for i in devices if i - distance in devices]
    return lax.ppermute(block, axis, route)


def linear_combine(earlier, later):
    return (earlier[0] * later[0], later[0] * earlier[1] + later[1])


def carry_pass(block_decay, summary, backward):
    identity = (jnp.ones_like(summary), jnp.zeros_like(summary))
    return prefix((block_decay, summary), "ctx", linear_combine, identity, backward)[1]


def local(projected, cotangent, conv_taps, residues, decay_rates, skip_gain):
    streams = projected[0]
    tok_rows = streams.shape[1]
    width = streams.shape[2]
    order = residues.shape[0]
    tap_count = conv_taps.shape[1]
    edge_rows = tap_count - 1
    prev_rows = shifted(streams[:, tok_rows - edge_rows :, :], "ctx", 1)
    padded = jnp.concatenate([prev_rows, streams], axis=1).astype(jnp.float32)
    features = conv_taps[:, 0, None, :] * padded[:, edge_rows : edge_rows + tok_rows, :]
    for offset in range(1, tap_count):
        features = (
            features
            + conv_taps[:, offset, None, :]
            * padded[:, edge_rows - offset : edge_rows - offset + tok_rows, :]
        )
    query = features[0]
    keyed = features[1]
    valued = features[2]
    drive = keyed * valued
    decays = jnp.exp(-decay_rates)
    root_norm = jnp.sqrt(-jnp.expm1(-2.0 * decay_rates))
    coeffs = residues * root_norm
    cot_rows = cotangent[0].astype(jnp.float32)
    grad_z = cot_rows * query
    zeros_state = jnp.zeros((order, width), jnp.float32)

    def local_step(carried, rows):
        state_now, adj_now = carried
        drive_row, grad_row = rows
        state_now = decays * state_now + drive_row[None, :]
        adj_now = decays * adj_now + coeffs * grad_row[None, :]
        return ((state_now, adj_now), None)

    (end_state, first_adjoint), _ = lax.scan(
        local_step, (zeros_state, zeros_state), (drive, grad_z[::-1]), unroll=8
    )
    block_decay = jnp.exp(-decay_rates * tok_rows)
    state_in = carry_pass(block_decay, end_state, False)
    adjoint_in = carry_pass(block_decay, first_adjoint, True)

    def forward_step(carried, rows):
        state_now, coeff_acc = carried
        drive_row, grad_row = rows
        before = state_now
        state_now = decays * state_now + drive_row[None, :]
        coeff_acc = coeff_acc + grad_row[None, :] * state_now
        return ((state_now, coeff_acc), (before, jnp.sum(coeffs * state_now, axis=0)))

    (_, coeff_grad), (state_prev, long_term) = lax.scan(
        forward_step, (state_in, zeros_state), (drive, grad_z), unroll=8
    )

    def backward_step(carried, rows):
        adj_now, decay_acc = carried
        grad_row, before = rows
        adj_now = decays * adj_now + coeffs * grad_row[None, :]
        decay_acc = decay_acc + adj_now * before
        return ((adj_now, decay_acc), jnp.sum(adj_now, axis=0))

    (_, decay_grad), adjoint_total = lax.scan(
        backward_step, (adjoint_in, zeros_state), (grad_z, state_prev), reverse=True, unroll=8
    )
    mixer_out = long_term + skip_gain * drive
    mixed = (query * mixer_out).astype(jnp.bfloat16)[None]
    grad_drive = adjoint_total + skip_gain * grad_z
    feature_grad = jnp.stack(
        [cot_rows * mixer_out, grad_drive * valued, grad_drive * keyed], axis=0
    )
    next_rows = shifted(feature_grad[:, :edge_rows, :], "ctx", -1)
    grad_padded = jnp.concatenate([feature_grad, next_rows], axis=1)
    stream_grad = conv_taps[:, 0, None, :] * grad_padded[:, 0:tok_rows, :]
    for offset in range(1, tap_count):
        stream_grad = (
            stream_grad
            + conv_taps[:, offset, None, :] * grad_padded[:, offset : offset + tok_rows, :]
        )
    input_grad = stream_grad.astype(jnp.bfloat16)[None]
    taps_grad = jnp.stack(
        [
            jnp.sum(
                feature_grad * padded[:, edge_rows - offset : edge_rows - offset + tok_rows, :],
                axis=1,
            )
            for offset in range(tap_count)
        ],
        axis=1,
    )
    skip_grad = jnp.sum(grad_z * drive, axis=0)
    residue_grad = coeff_grad * root_norm
    rate_grad = -decays * decay_grad + coeff_grad * residues * decays * decays / root_norm
    grad_sums = lax.psum((taps_grad, residue_grad, rate_grad, skip_grad), ("dp", "ctx"))
    totals = lax.psum(tuple((jnp.sum(member * member) for member in grad_sums)), "tp")
    full_width = width * lax.axis_size("tp")
    entries = (3 * tap_count * full_width, order * full_width, order * full_width, full_width)
    updates = [
        member / jnp.maximum(1.0, jnp.sqrt(total / entry_count))
        for member, total, entry_count in zip(grad_sums, totals, entries)
    ]
    return (mixed, input_grad, updates[0], updates[1], updates[2], updates[3])


LANES = 128
SUBL = 8
HALO = 8
GROUP = 4
GRANT = 62 * 1024 * 1024
MESH = pl.DeviceIdType.MESH
F32 = jnp.float32


def iota_rows():
    return lax.broadcasted_iota(jnp.int32, (SUBL, LANES), 0)


def mega(sizes, x_hbm, cot_hbm, taps_hbm, res_hbm, rate_hbm, skip_hbm,
         mixed_hbm, ig_hbm, taps_upd, res_upd, rate_upd, skip_upd,
         x, cot, taps, res, rate, skip, load_sem, mixed, ig, out_sem, prev, nxt, nct, xs, ct, feat, drive, gz, pre_f, pre_b, sum_f, sum_b, got_f, got_b,
         tab, in_f, in_b, lt, at, hist, acc_c, acc_d, ms, fg, grads, rs, ag, tot, tot_tp, tot_all,
         halo_send, halo_recv, f_send, f_recv, b_send, b_recv,
         rs_send, rs_recv, ag_send, ag_recv, tp_send, tp_recv, all_send, all_recv):
    ndp, nctx, ntp, order, tap_count = sizes
    tok, width = cot.shape
    blocks = width // LANES
    group = ndp * nctx
    seg = (tok + HALO) // SUBL
    last = seg - 1 - HALO
    grad_rows = grads.shape[1]
    me_dp = lax.axis_index("dp")
    me = lax.axis_index("ctx")
    me_tp = lax.axis_index("tp")
    me_g = me_dp * nctx + me

    def peer(p):
        return {"dp": p // nctx, "ctx": lax.rem(p, nctx)}

    pairs = ((rate_hbm, rate), (x_hbm, x), (cot_hbm, cot), (res_hbm, res), (taps_hbm, taps), (skip_hbm, skip))
    loads = [pltpu.make_async_copy(src, dst, load_sem.at[k]) for k, (src, dst) in enumerate(pairs)]
    for load in loads:
        load.start()
    barrier = pltpu.get_barrier_semaphore()
    for k in range(1, group):
        p = lax.rem(me_g + k, group)
        pl.semaphore_signal(barrier, inc=1, device_id=peer(p), device_id_type=MESH)
    for k in range(1, ntp):
        q = lax.rem(me_tp + k, ntp)
        pl.semaphore_signal(barrier, inc=1, device_id={"tp": q}, device_id_type=MESH)
    def lanes(b):
        return pl.ds(pl.multiple_of(b * LANES, LANES), LANES)

    def row(ref, n, b):
        return jnp.broadcast_to(ref[pl.ds(n, 1), lanes(b)], (SUBL, LANES))

    def trow(k, b, n):
        return jnp.broadcast_to(tab[k, b, pl.ds(n, 1), :], (SUBL, LANES))

    def at_j(j):
        return pl.ds(j * SUBL, SUBL)

    def strided(j):
        return pl.ds(j, SUBL, stride=seg)

    def turn(i):
        return lax.rem(i + me_dp * (blocks // ndp), blocks)

    for load in loads:
        load.wait()

    def fill(b, carry):
        lo = lanes(b)
        rates = rate[:, lo]
        tab[0, b] = jnp.exp(-rates)
        tab[1, b] = jnp.exp(-rates * seg)
        tab[2, b] = jnp.exp(-rates * (2 * seg))
        tab[3, b] = jnp.exp(-rates * (4 * seg))
        tab[4, b] = jnp.exp(-rates * (seg - HALO))
        twice = 2.0 * rates
        series = jnp.ones_like(twice)
        for k in range(12, 1, -1):
            series = 1.0 - twice * series * (1.0 / k)
        root = jnp.sqrt(jnp.where(twice < 0.5, twice * series, 1.0 - jnp.exp(-twice)))
        tab[5, b] = root
        tab[6, b] = res[:, lo] * root
        tab[7, b] = rates
        for s in range(3):
            for r in range(tok // 16):
                xs[b, s, HALO + 16 * r : HALO + 16 * r + 16, :] = x[s, 16 * r : 16 * r + 16, lo].astype(F32)
        for r in range(tok // 16):
            ct[b, 16 * r : 16 * r + 16, :] = cot[16 * r : 16 * r + 16, lo].astype(F32)
        return carry

    lax.fori_loop(0, blocks // 2, fill, 0)
    pl.semaphore_wait(barrier, group - 1 + ntp - 1)

    def remote(src, dst, send, recv, where):
        return pltpu.make_async_remote_copy(
            src_ref=src, dst_ref=dst, send_sem=send, recv_sem=recv,
            device_id=where, device_id_type=MESH)

    down = remote(x_hbm.at[:, pl.ds(tok - HALO, HALO), :], prev, halo_send.at[0], halo_recv.at[0],
                  {"ctx": jnp.minimum(me + 1, nctx - 1)})
    up = remote(x_hbm.at[:, pl.ds(0, HALO), :], nxt, halo_send.at[1], halo_recv.at[1],
                {"ctx": jnp.maximum(me - 1, 0)})
    upc = remote(cot_hbm.at[pl.ds(0, HALO), :], nct, halo_send.at[2], halo_recv.at[2],
                 {"ctx": jnp.maximum(me - 1, 0)})

    @pl.when(me < nctx - 1)
    def _():
        down.start()

    @pl.when(me > 0)
    def _():
        up.start()
        upc.start()

    @pl.when(me == 0)
    def _():
        prev[...] = jnp.zeros_like(prev)

    @pl.when(me == nctx - 1)
    def _():
        nxt[...] = jnp.zeros_like(nxt)
        nct[...] = jnp.zeros_like(nct)

    lax.fori_loop(blocks // 2, blocks, fill, 0)

    @pl.when(me > 0)
    def _():
        down.wait_recv()

    @pl.when(me < nctx - 1)
    def _():
        up.wait_recv()
        upc.wait_recv()

    def f_copy(b, far):
        return remote(sum_f.at[b], got_f.at[far - 1, b], f_send.at[far - 1, b], f_recv.at[far - 1, b],
                      {"ctx": jnp.minimum(me + far, nctx - 1)})

    def b_copy(b, far):
        return remote(sum_b.at[b], got_b.at[far - 1, b], b_send.at[far - 1, b], b_recv.at[far - 1, b],
                      {"ctx": jnp.maximum(me - far, 0)})

    def first(i, carry):
        b = turn(i)
        lo = lanes(b)
        for s in range(3):
            xs[b, s, 0:HALO, :] = prev[s, :, lo].astype(F32)
            xs[b, s, tok + HALO : tok + 2 * HALO, :] = nxt[s, :, lo].astype(F32)
        ct[b, tok : tok + HALO, :] = nct[:, lo].astype(F32)
        for s in range(3):
            w = [jnp.broadcast_to(taps[s, o : o + 1, lo], (SUBL, LANES)) for o in range(tap_count)]
            for j in range(seg):
                total = w[0] * xs[b, s, strided(HALO + j), :]
                for o in range(1, tap_count):
                    total = total + w[o] * xs[b, s, strided(HALO + j - o), :]
                feat[b, s, at_j(j), :] = total
                if s == 0:
                    gz[b, at_j(j), :] = total * ct[b, strided(j), :]
                if s == 2:
                    drive[b, at_j(j), :] = total * feat[b, 1, at_j(j), :]
        rows_at = iota_rows()

        def modes(g, c):
            ns = [g * GROUP + m for m in range(GROUP)]
            d = [trow(0, b, n) for n in ns]
            s = [drive[b, at_j(0), :]] * GROUP
            a = [gz[b, at_j(seg - 1), :]] * GROUP
            mid_s = s if last == 0 else None
            mid_a = a if seg - 1 == HALO else None
            for j in range(1, seg):
                dr = drive[b, at_j(j), :]
                gr = gz[b, at_j(seg - 1 - j), :]
                s = [d[m] * s[m] + dr for m in range(GROUP)]
                a = [d[m] * a[m] + gr for m in range(GROUP)]
                if j == last:
                    mid_s = s
                if seg - 1 - j == HALO:
                    mid_a = a
            for m, n in enumerate(ns):
                y, z = s[m], a[m]
                for k, far in ((1, 1), (2, 2), (3, 4)):
                    p = trow(k, b, n)
                    y = y + jnp.where(rows_at >= far, p * pltpu.roll(y, far, 0), 0.0)
                    z = z + jnp.where(rows_at < SUBL - far, p * pltpu.roll(z, SUBL - far, 0), 0.0)
                y = jnp.where(rows_at >= 1, pltpu.roll(y, 1, 0), 0.0)
                z = jnp.where(rows_at < SUBL - 1, pltpu.roll(z, SUBL - 1, 0), 0.0)
                pre_f[b, n] = y
                pre_b[b, n] = z
                p = trow(4, b, n)
                sum_f[b, pl.ds(n, 1), :] = (mid_s[m] + p * y)[SUBL - 1 : SUBL, :]
                sum_b[b, pl.ds(n, 1), :] = (mid_a[m] + p * z)[0:1, :]
            return c

        lax.fori_loop(0, order // GROUP, modes, 0)
        for far in range(1, nctx):
            @pl.when(me + far < nctx)
            def _():
                f_copy(b, far).start()

            @pl.when(me >= far)
            def _():
                b_copy(b, far).start()
        return carry

    lax.fori_loop(0, blocks, first, 0)

    def rs_copy(b):
        return remote(grads.at[b], rs.at[me_g], rs_send.at[b], rs_recv.at[me_g], peer(b))

    def out_copies(b):
        lo = lanes(b)
        return (pltpu.make_async_copy(mixed.at[:, lo], mixed_hbm.at[:, lo], out_sem.at[0, b]),
                pltpu.make_async_copy(ig.at[:, :, lo], ig_hbm.at[:, :, lo], out_sem.at[1, b]))

    def second(i, carry):
        b = turn(i)
        lo = lanes(b)
        rates = rate[:, lo]
        in_f[...] = jnp.zeros_like(in_f)
        in_b[...] = jnp.zeros_like(in_b)
        for far in range(1, nctx):
            scale = jnp.exp(-rates * (tok * (far - 1)))

            @pl.when(me >= far)
            def _():
                f_copy(b, far).wait_recv()
                in_f[...] += scale * got_f[far - 1, b]

            @pl.when(me + far < nctx)
            def _():
                b_copy(b, far).wait_recv()
                in_b[...] += scale * got_b[far - 1, b]
        lt[...] = jnp.zeros_like(lt)
        at[...] = jnp.zeros_like(at)
        rows_at = iota_rows()
        seg_f = rows_at.astype(F32) * (-float(seg))
        seg_b = (SUBL - 1 - rows_at).astype(F32) * (-float(seg))
        zero = jnp.zeros((SUBL, LANES), F32)

        def fold(head, rest):
            return jnp.sum(head + jnp.where(rows_at < SUBL - 1, rest, 0.0), axis=0, keepdims=True)

        def modes(g, carried):
            ns = [g * GROUP + m for m in range(GROUP)]
            d = [trow(0, b, n) for n in ns]
            c = [trow(6, b, n) for n in ns]
            rr = [trow(7, b, n) for n in ns]
            s = [pre_f[b, n] + jnp.exp(seg_f * rr[m]) * jnp.broadcast_to(in_f[pl.ds(n, 1), :], (SUBL, LANES))
                 for m, n in enumerate(ns)]
            a = [pre_b[b, n] + jnp.exp(seg_b * rr[m]) * jnp.broadcast_to(in_b[pl.ds(n, 1), :], (SUBL, LANES))
                 for m, n in enumerate(ns)]
            head, rest = [zero] * GROUP, [zero] * GROUP
            for j in range(seg):
                dr = drive[b, at_j(j), :]
                gr = gz[b, at_j(j), :]
                for m in range(GROUP):
                    hist[m, j] = s[m]
                s = [d[m] * s[m] + dr for m in range(GROUP)]
                out = lt[at_j(j), :]
                for m in range(GROUP):
                    out = out + c[m] * s[m]
                lt[at_j(j), :] = out
                if j <= last:
                    head = [head[m] + gr * s[m] for m in range(GROUP)]
                else:
                    rest = [rest[m] + gr * s[m] for m in range(GROUP)]
            for m, n in enumerate(ns):
                acc_c[pl.ds(n, 1), :] = fold(head[m], rest[m])
            head, rest = [zero] * GROUP, [zero] * GROUP
            for j in reversed(range(seg)):
                gr = gz[b, at_j(j), :]
                a = [d[m] * a[m] + gr for m in range(GROUP)]
                out = at[at_j(j), :]
                for m in range(GROUP):
                    out = out + c[m] * a[m]
                at[at_j(j), :] = out
                if j <= last:
                    head = [head[m] + a[m] * hist[m, j] for m in range(GROUP)]
                else:
                    rest = [rest[m] + a[m] * hist[m, j] for m in range(GROUP)]
            for m, n in enumerate(ns):
                acc_d[pl.ds(n, 1), :] = fold(head[m], rest[m])
            return carried

        lax.fori_loop(0, order // GROUP, modes, 0)
        decays, root, coeffs = tab[0, b], tab[5, b], tab[6, b]
        coeff_grad = acc_c[...]
        grads[b, 0:order, :] = coeff_grad * root
        grads[b, order : 2 * order, :] = (
            -decays * (coeffs * acc_d[...]) + coeff_grad * res[:, lo] * decays * decays / root)
        gain = row(skip, 0, b)
        head, rest = zero, zero
        for j in range(seg):
            dr = drive[b, at_j(j), :]
            gr = gz[b, at_j(j), :]
            mixer = lt[at_j(j), :] + gain * dr
            ms[strided(j), :] = feat[b, 0, at_j(j), :] * mixer
            fg[0, strided(j), :] = ct[b, strided(j), :] * mixer
            grad_drive = at[at_j(j), :] + gain * gr
            fg[1, strided(j), :] = grad_drive * feat[b, 2, at_j(j), :]
            fg[2, strided(j), :] = grad_drive * feat[b, 1, at_j(j), :]
            if j <= last:
                head = head + gr * dr
            else:
                rest = rest + gr * dr
        base = 2 * order
        grads[b, base + 3 * tap_count : base + 3 * tap_count + 1, :] = fold(head, rest)
        pad = grad_rows - (base + 3 * tap_count + 1)
        grads[b, base + 3 * tap_count + 1 : grad_rows, :] = jnp.zeros((pad, LANES), F32)
        for r in range(tok // 16):
            mixed[16 * r : 16 * r + 16, lo] = ms[16 * r : 16 * r + 16, :].astype(mixed.dtype)
        for s in range(3):
            w = [jnp.broadcast_to(taps[s, o : o + 1, lo], (SUBL, LANES)) for o in range(tap_count)]
            sums = [zero] * tap_count
            for r in range(tok // 16):
                parts = []
                for half in range(2):
                    at_row = 16 * r + 8 * half
                    here = fg[s, at_row : at_row + SUBL, :]
                    total = w[0] * here
                    sums[0] = sums[0] + here * xs[b, s, HALO + at_row : HALO + at_row + SUBL, :]
                    for o in range(1, tap_count):
                        total = total + w[o] * fg[s, at_row + o : at_row + o + SUBL, :]
                        sums[o] = sums[o] + here * xs[b, s, HALO + at_row - o : HALO + at_row - o + SUBL, :]
                    parts.append(total)
                ig[s, 16 * r : 16 * r + 16, lo] = jnp.concatenate(parts, axis=0).astype(ig.dtype)
            for o in range(tap_count):
                at_out = base + s * tap_count + o
                grads[b, at_out : at_out + 1, :] = jnp.sum(sums[o], axis=0, keepdims=True)

        @pl.when(b != me_g)
        def _():
            rs_copy(b).start()

        for copy in out_copies(b):
            copy.start()
        return carry

    lax.fori_loop(0, blocks, second, 0)

    others = [lax.rem(me_g + k, group) for k in range(1, group)]
    total = grads[me_g]
    for p in others:
        remote(grads.at[p], rs.at[p], rs_send.at[p], rs_recv.at[p], peer(p)).wait_recv()
        total = total + rs[p]
    ag[me_g] = total
    for p in others:
        remote(ag.at[me_g], ag.at[me_g], ag_send.at[p], ag_recv.at[me_g], peer(p)).start()
    square = total * total
    res_sq = jnp.sum(square[0:order, :], axis=0, keepdims=True)
    rate_sq = jnp.sum(square[order : 2 * order, :], axis=0, keepdims=True)
    skip_at = 2 * order + 3 * tap_count
    skip_sq = square[skip_at : skip_at + 1, :]
    rest_sq = jnp.sum(
        jnp.where(lax.broadcasted_iota(jnp.int32, (grad_rows - 2 * order, LANES), 0) < 3 * tap_count,
                  square[2 * order :, :], 0.0), axis=0, keepdims=True)
    rows_at = iota_rows()
    tile = jnp.where(rows_at == 0, res_sq, jnp.where(rows_at == 1, rate_sq,
                     jnp.where(rows_at == 2, rest_sq, jnp.where(rows_at == 3, skip_sq, 0.0))))
    tot[...] = tile
    tps = [lax.rem(me_tp + k, ntp) for k in range(1, ntp)]
    for q in tps:
        remote(tot, tot_tp.at[me_tp], tp_send.at[q], tp_recv.at[me_tp], {"tp": q}).start()
    for q in tps:
        remote(tot, tot_tp.at[q], tp_send.at[q], tp_recv.at[q], {"tp": q}).wait_recv()
        tile = tile + tot_tp[q]
    tot_all[me_g] = tile
    for p in others:
        remote(tot_all.at[me_g], tot_all.at[me_g], all_send.at[p], all_recv.at[me_g], peer(p)).start()
    for p in others:
        remote(tot_all.at[p], tot_all.at[p], all_send.at[p], all_recv.at[p], peer(p)).wait_recv()
        tile = tile + tot_all[p]
    sums = jnp.sum(tile, axis=1, keepdims=True)
    full = width * ntp
    counts = (order * full, order * full, 3 * tap_count * full, full)
    scales = [1.0 / jnp.maximum(1.0, jnp.sqrt(sums[k : k + 1, :] * (1.0 / counts[k]))) for k in range(4)]
    which = lax.broadcasted_iota(jnp.int32, (grad_rows, 1), 0)
    scale = jnp.where(which < order, scales[0], jnp.where(which < 2 * order, scales[1],
                      jnp.where(which < skip_at, scales[2], scales[3])))
    scale = jnp.broadcast_to(scale, (grad_rows, LANES))
    def write(p):
        lo = lanes(p)
        block = ag[p] * scale
        res_upd[:, lo] = block[0:order, :]
        rate_upd[:, lo] = block[order : 2 * order, :]
        for s in range(3):
            at_row = 2 * order + s * tap_count
            taps_upd[s, :, lo] = block[at_row : at_row + tap_count, :]
        skip_upd[:, lo] = block[skip_at : skip_at + 1, :]

    write(me_g)
    for p in others:
        remote(ag.at[p], ag.at[p], ag_send.at[p], ag_recv.at[p], peer(p)).wait_recv()
        write(p)

    @pl.when(me < nctx - 1)
    def _():
        down.wait_send()

    @pl.when(me > 0)
    def _():
        up.wait_send()
        upc.wait_send()

    def drain(b, carry):
        for copy in out_copies(b):
            copy.wait()
        for far in range(1, nctx):
            @pl.when(me + far < nctx)
            def _():
                f_copy(b, far).wait_send()

            @pl.when(me >= far)
            def _():
                b_copy(b, far).wait_send()
        return carry

    lax.fori_loop(0, blocks, drain, 0)
    for p in others:
        rs_copy(p).wait_send()
        remote(ag.at[me_g], ag.at[me_g], ag_send.at[p], ag_recv.at[me_g], peer(p)).wait_send()
        remote(tot_all.at[me_g], tot_all.at[me_g], all_send.at[p], all_recv.at[me_g], peer(p)).wait_send()
    for q in tps:
        remote(tot, tot_tp.at[me_tp], tp_send.at[q], tp_recv.at[me_tp], {"tp": q}).wait_send()


def place(*refs):
    sem = refs[-1]
    copies = [pltpu.make_async_copy(refs[k], refs[6 + k], sem.at[k]) for k in range(6)]
    for copy in copies:
        copy.start()
    for copy in copies:
        copy.wait()


def fused(projected, cotangent, conv_taps, residues, decay_rates, skip_gain):
    ndp, nctx, ntp = (lax.axis_size(a) for a in ("dp", "ctx", "tp"))
    _, _, tok, width = projected.shape
    order = residues.shape[0]
    tap_count = conv_taps.shape[1]
    blocks = width // LANES
    group = ndp * nctx
    seg = (tok + HALO) // SUBL
    grad_rows = -(-(2 * order + 3 * tap_count + 1) // SUBL) * SUBL
    vm = pl.BlockSpec(memory_space=pltpu.VMEM)
    dma = pltpu.SemaphoreType.DMA
    V = pltpu.VMEM
    bf = jnp.bfloat16
    shapes = (
        jax.ShapeDtypeStruct((tok, width), bf),
        jax.ShapeDtypeStruct((3, tok, width), bf),
        jax.ShapeDtypeStruct((3, tap_count, width), F32),
        jax.ShapeDtypeStruct((order, width), F32),
        jax.ShapeDtypeStruct((order, width), F32),
        jax.ShapeDtypeStruct((1, width), F32),
    )
    hbm = pl.BlockSpec(memory_space=pltpu.HBM)
    parts = pl.pallas_call(
        functools.partial(mega, (ndp, nctx, ntp, order, tap_count)),
        out_shape=shapes,
        in_specs=[hbm] * 6,
        out_specs=(hbm, hbm, vm, vm, vm, vm),
        scratch_shapes=[
            V((3, tok, width), bf), V((tok, width), bf), V((3, tap_count, width), F32),
            V((order, width), F32), V((order, width), F32), V((1, width), F32), dma((6,)),
            V((tok, width), bf), V((3, tok, width), bf), dma((2, blocks)),
            V((3, HALO, width), bf), V((3, HALO, width), bf), V((HALO, width), bf),
            V((blocks, 3, tok + 2 * HALO, LANES), F32), V((blocks, tok + HALO, LANES), F32),
            V((blocks, 3, seg * SUBL, LANES), F32), V((blocks, seg * SUBL, LANES), F32),
            V((blocks, seg * SUBL, LANES), F32),
            V((blocks, order, SUBL, LANES), F32), V((blocks, order, SUBL, LANES), F32),
            V((blocks, order, LANES), F32), V((blocks, order, LANES), F32),
            V((nctx - 1, blocks, order, LANES), F32), V((nctx - 1, blocks, order, LANES), F32),
            V((8, blocks, order, LANES), F32), V((order, LANES), F32), V((order, LANES), F32),
            V((seg * SUBL, LANES), F32), V((seg * SUBL, LANES), F32),
            V((GROUP, seg, SUBL, LANES), F32), V((order, LANES), F32), V((order, LANES), F32),
            V((seg * SUBL, LANES), F32), V((3, seg * SUBL, LANES), F32),
            V((blocks, grad_rows, LANES), F32), V((group, grad_rows, LANES), F32),
            V((group, grad_rows, LANES), F32),
            V((SUBL, LANES), F32), V((ntp, SUBL, LANES), F32), V((group, SUBL, LANES), F32),
            dma((3,)), dma((3,)),
            dma((nctx - 1, blocks)), dma((nctx - 1, blocks)), dma((nctx - 1, blocks)), dma((nctx - 1, blocks)),
            dma((group,)), dma((group,)), dma((group,)), dma((group,)),
            dma((ntp,)), dma((ntp,)), dma((group,)), dma((group,)),
        ],
        compiler_params=pltpu.CompilerParams(
            collective_id=0, has_side_effects=True, vmem_limit_bytes=GRANT),
    )(projected[0], cotangent[0], conv_taps, residues, decay_rates, skip_gain.reshape(1, width))
    mixed, ig, taps_upd, res_upd, rate_upd, skip_upd = pl.pallas_call(
        place,
        out_shape=shapes,
        in_specs=[vm] * 6,
        out_specs=(hbm,) * 6,
        scratch_shapes=[dma((6,))],
    )(*parts)
    return mixed[None], ig[None], taps_upd, res_upd, rate_upd, skip_upd.reshape(width)


def fits(mesh, projected, residues, conv_taps):
    tok = projected.shape[2] // mesh.shape["ctx"]
    width = projected.shape[3] // mesh.shape["tp"]
    group = mesh.shape["dp"] * mesh.shape["ctx"]
    return (width == group * LANES and tok % 16 == 0 and tok >= 64 and mesh.shape["ctx"] > 1
            and mesh.shape["tp"] > 1 and residues.shape[0] % SUBL == 0
            and conv_taps.shape[1] <= HALO - 1 and projected.shape[0] == mesh.shape["dp"])


def solution(mesh):
    in_specs = (
        P("dp", None, "ctx", "tp"),
        P("dp", "ctx", "tp"),
        P(None, None, "tp"),
        P(None, "tp"),
        P(None, "tp"),
        P("tp"),
    )
    out_specs = (
        P("dp", "ctx", "tp"),
        P("dp", None, "ctx", "tp"),
        P(None, None, "tp"),
        P(None, "tp"),
        P(None, "tp"),
        P("tp"),
    )

    def run(projected, cotangent, conv_taps, residues, decay_rates, skip_gain):
        body = fused if fits(mesh, projected, residues, conv_taps) else local
        mapped = jax.shard_map(body, mesh=mesh, in_specs=in_specs, out_specs=out_specs, check_vma=False)
        return mapped(projected, cotangent, conv_taps, residues, decay_rates, skip_gain)

    return run
```
